32 devices in a mesh: shot: 4 (over z), slab: 8 (over y, x, core).
Axes of the slice: x: 2, y: 2, z: 4, core: 2. Of those that a mesh axis runs over, the one named last changes fastest.
Arguments:
- source_field: bfloat16 [4, 256, 384, 512], P('shot', 'slab'), may hold values from -6 to 6
- receiver_fields: bfloat16 [8, 256, 384, 512], P('shot', 'slab'), may hold values from -6 to 6
- weights: int32 [8], P('shot'), may hold values from -1 to 1, as said below
- model: bfloat16 [256, 384, 512], P(('slab', 'shot')), may hold values from -6 to 6
- wedge_sizes: int32 [16], replicated, may hold values from 1 to 95, as said below
- wedge_scales: float32 [16], replicated, may hold values from 0.3 to 3
Outputs:
- new_model: float32 [256, 384, 512], P(('slab', 'shot'))
The draws below stay inside these ranges and needn't reach their ends.
Inputs may be any that keep to these rules, and one draw needn't show every extreme that they name: `weights`: each weight is -1 or +1. `wedge_sizes`: wedges 2d and 2d + 1 together hold either 512 // 8 // 2 or 96 columns, each count for half of the pairs; every wedge holds one column or more; all sizes sum to 512.
All inputs are finite; a program needn't handle non-finite values.
Results may differ from the reference program's by a relative error of at most 0.0003.
Values sent between devices are 32-bit elements; how exact they have to be, the bound alone decides.
A program may use at most 128 MiB of HBM per device.

```python
import math
import jax
import jax.numpy as jnp
from jax import lax

NZ = 256
NY = 384
NX = 512
SH_DEV = 2
GROUPS = 4
SHOTS = 8
NWEDGE = 16
N_SHOT = 4
N_SLAB = 8


def draw_weights(key, part):
    return 2 * jax.random.randint(key, (SH_DEV * N_SHOT,), 0, 2, dtype=jnp.int32) - 1


def draw_wedge_sizes(key, part):
    first_key = jax.random.fold_in(key, 11)
    second_key = jax.random.fold_in(key, 23)
    share = NX // N_SLAB
    half = N_SLAB // 2
    pattern = jnp.concatenate([jnp.full((half,), share // 2, jnp.int32), jnp.full((N_SLAB - half,), 3 * share // 2, jnp.int32)])
    totals = pattern[jax.random.permutation(first_key, N_SLAB)]
    raw = jax.random.randint(second_key, (N_SLAB,), 0, 1 << 20, dtype=jnp.int32)
    leading = 1 + raw % jnp.maximum(totals - 1, 1)
    trailing = totals - leading
    return jnp.stack([leading, trailing], axis=1).reshape(-1).astype(jnp.int32)


def level_of(own_key, shape, shards, low, top_value):
    factor_of = 1.0
    for dim, shards_of in shards:
        draws = jax.random.uniform(jax.random.fold_in(jax.random.fold_in(own_key, 6), dim), (shards_of,), jnp.float32, low / len(shards), top_value / len(shards))
        factor_of = factor_of * jnp.repeat(jnp.exp(draws), shape[dim] // shards_of).reshape((-1,) + (1,) * (len(shape) - 1 - dim))
    return factor_of


def noise(stream_key, dims, width, bound, split=(), kind=jnp.bfloat16):
    gain = level_of(stream_key, dims, split, -0.22, 0.18) if split else 1.0
    drawn = jax.random.normal(stream_key, dims, jnp.float32) * width * gain
    return jnp.minimum(jnp.maximum(drawn, -bound), bound).astype(kind)


def setup_inputs(seed: int = 0) -> dict:
    keys = jax.random.split(jax.random.key(seed), 7)
    return {
        "source_field": noise(keys[0], (GROUPS, NZ, NY, NX), 1.0, 6.0, ((0, 4), (1, 8))),
        "receiver_fields": noise(keys[1], (SHOTS, NZ, NY, NX), 1.0, 6.0, ((0, 4), (1, 8))),
        "weights": draw_weights(jax.random.fold_in(keys[6], 71), 0),
        "model": noise(keys[3], (NZ, NY, NX), 1.0, 6.0, ((0, 32),)),
        "wedge_sizes": draw_wedge_sizes(jax.random.fold_in(keys[6], 71), 0),
        "wedge_scales": jnp.clip(jnp.exp(jax.random.uniform(keys[5], (NWEDGE,), jnp.float32, math.log(0.3), math.log(3.0))), 0.3, 3.0),
    }


STEP_SIZE = 0.25
EPSILON = 1e-06

def reference(source_field, receiver_fields, weights, model, wedge_sizes, wedge_scales):
    groups = source_field.shape[0]
    per_group = receiver_fields.shape[0] // groups
    signs = weights.astype(jnp.float32).reshape(groups, per_group)
    receivers = receiver_fields.reshape((groups, per_group) + receiver_fields.shape[1:])

    def add_group(total, inputs):
        source, group_fields, group_signs = inputs
        encoded = jnp.zeros(source.shape, jnp.float32)
        for member in range(per_group):
            encoded = encoded + group_signs[member] * group_fields[member].astype(jnp.float32)
        return (total + source.astype(jnp.float32) * encoded, None)
    gradient, _ = lax.scan(add_group, jnp.zeros(model.shape, jnp.float32), (source_field, receivers, signs))
    update = model.astype(jnp.float32) - STEP_SIZE * gradient
    spectrum = jnp.fft.fftn(update)
    depth, rows, columns = update.shape
    ends = jnp.cumsum(wedge_sizes).astype(jnp.int32)
    starts = (ends - wedge_sizes).astype(jnp.int32)
    column = jnp.arange(columns, dtype=jnp.int32)
    member_of = ((column[:, None] >= starts[None, :]) & (column[:, None] < ends[None, :])).astype(jnp.float32)
    energy = jnp.real(spectrum) ** 2 + jnp.imag(spectrum) ** 2
    column_power = lax.optimization_barrier(jnp.sum(energy, axis=(0, 1)))
    wedge_power = jnp.dot(column_power, member_of, precision=lax.Precision.HIGHEST)
    entries = wedge_sizes.astype(jnp.float32) * (depth * rows)
    spread = jnp.sqrt(wedge_power / entries + EPSILON)
    level = jnp.dot(member_of, wedge_scales * spread, precision=lax.Precision.HIGHEST)
    magnitude = jnp.sqrt(energy)
    factor = jnp.maximum(magnitude - level, 0.0) / jnp.maximum(magnitude, level)
    return jnp.real(jnp.fft.ifftn(spectrum * factor)).astype(jnp.float32)
```

```python
import functools

import jax
import jax.numpy as jnp
import numpy as np
from jax import lax
from jax.experimental import pallas as pl
from jax.experimental.pallas import tpu as pltpu
from jax.sharding import PartitionSpec as P

STEP_SIZE = 0.25
EPSILON = 1e-06
HIGHEST = lax.Precision.HIGHEST
CHUNKS = 4
F32 = jnp.float32
BF16 = jnp.bfloat16


def halves(x):
    high = x.astype(BF16)
    return high, (x - high.astype(F32)).astype(BF16)


def host_halves(table):
    table = table.astype(np.float32)
    high = table.astype(BF16)
    low = (table - high.astype(np.float32)).astype(BF16)
    return jnp.asarray(np.stack([high, low]))


def dot3(a, b, dims=((1,), (0,))):
    product = functools.partial(
        lax.dot_general, dimension_numbers=(dims, ((), ())), preferred_element_type=F32
    )
    return product(a[0], b[0]) + (product(a[0], b[1]) + product(a[1], b[0]))


def circle(rows, columns, length):
    angle = (np.outer(rows, columns) % length) * (2.0 * np.pi / length)
    return np.cos(angle), np.sin(angle)


def x_table(shots, slabs, width):
    slots = width // 2 // (shots * slabs)
    cosine, sine = circle(np.arange(width // 2), np.arange(width), width)
    sine = -sine
    sine[0] = 1.0 - 2.0 * (np.arange(width) % 2)
    shape = (shots * slabs, slots, width)
    return np.stack([cosine.reshape(shape), sine.reshape(shape)], axis=1).reshape(width, width)


def forward_x(shots, planes, first, sign_ref, shot_ref, source_ref, recv_ref, model_ref, tx_ref, out_ref):
    encoded = jnp.zeros(source_ref.shape[1:], F32)
    for member in range(recv_ref.shape[0]):
        encoded = encoded + sign_ref[member].astype(F32) * recv_ref[member, 0].astype(F32)
    plane = pl.program_id(0) + first
    own = (plane // planes == shot_ref[0]).astype(F32)
    part = own * model_ref[0].astype(F32) - STEP_SIZE * (source_ref[0].astype(F32) * encoded)
    result = dot3((tx_ref[0], tx_ref[1]), halves(part), ((1,), (1,)))
    rows = result.shape[0] // shots
    for shot in range(shots):
        out_ref[shot, 0] = result[shot * rows : (shot + 1) * rows]


def forward_y(slabs, in_ref, ty_ref, out_ref):
    depth, rows, width = in_ref.shape
    slots = rows // slabs // 2
    result = dot3(halves(in_ref[...].reshape(depth * rows, width)), (ty_ref[0], ty_ref[1]))
    with_cos, with_sin = result[:, :width], result[:, width:]
    for z in range(depth):
        for slab in range(slabs):
            re = z * rows + slab * 2 * slots
            im = re + slots
            out_ref[slab, z, 0] = with_cos[re : re + slots] + with_sin[im : im + slots]
            out_ref[slab, z, 1] = with_cos[im : im + slots] - with_sin[re : re + slots]


def forward_z(slots, packed_ref, tz_ref, *refs):
    pieces, (out_ref, middle_ref, power_ref) = refs[:CHUNKS], refs[CHUNKS:]
    slot = pl.program_id(0)
    depth = tz_ref.shape[2]

    def load(part):
        return jnp.concatenate([piece[part, 0] for piece in pieces], axis=0)

    def transform(re, im):
        width = re.shape[1]
        result = dot3((tz_ref[0], tz_ref[1]), halves(jnp.concatenate([re, im], axis=1)))
        with_cos, with_sin = result[:depth], result[depth:]
        return (
            with_cos[:, :width] + with_sin[:, width:],
            with_cos[:, width:] - with_sin[:, :width],
        )

    re_in, im_in = load(0), load(1)
    re, im = transform(re_in, im_in)
    out_ref[0, 0] = re
    out_ref[0, 1] = im
    power_ref[slot] = jnp.sum(re * re + im * im)

    @pl.when(slot == 0)
    def _():
        width = re.shape[1]
        sums = lax.broadcasted_iota(jnp.int32, (width, width), 0) + lax.broadcasted_iota(
            jnp.int32, (width, width), 1
        )
        mirror = ((sums == 0) | (sums == width)).astype(F32).astype(BF16)

        def flip(x):
            high, low = halves(x)
            return jnp.dot(high, mirror, preferred_element_type=F32) + jnp.dot(
                low, mirror, preferred_element_type=F32
            )

        other_re, other_im = transform(flip(re_in), -flip(im_in))
        flag = packed_ref[0] != 0
        first_re = jnp.where(flag, 0.5 * (re + other_re), re)
        first_im = jnp.where(flag, 0.5 * (im + other_im), im)
        last_re = jnp.where(flag, 0.5 * (im - other_im), 0.0)
        last_im = jnp.where(flag, 0.5 * (other_re - re), 0.0)
        out_ref[0, 0] = first_re
        out_ref[0, 1] = first_im
        middle_ref[0] = last_re
        middle_ref[1] = last_im
        power_ref[0] = jnp.sum(first_re * first_re + first_im * first_im)
        power_ref[slots] = jnp.sum(last_re * last_re + last_im * last_im)


def shrink_back(slots, level_ref, scale_ref, tz_ref, ty_ref, spec_ref, middle_ref, out_ref, held_ref):
    slot = pl.program_id(0)
    depth, width = spec_ref.shape[2:]

    def shrunk(re, im, index):
        magnitude = jnp.sqrt(re * re + im * im)
        total = 0.0
        for side in range(2):
            level = level_ref[side, index]
            total = total + jnp.maximum(magnitude - level, 0.0) / jnp.maximum(magnitude, level)
        total = total * scale_ref[index]
        return re * total, im * total

    re, im = shrunk(spec_ref[0, 0], spec_ref[0, 1], slot)
    held_ref[0] = re
    held_ref[1] = im

    @pl.when(slot == 0)
    def _():
        last_re, last_im = shrunk(middle_ref[0], middle_ref[1], slots)
        held_ref[0] = held_ref[0] - last_im
        held_ref[1] = held_ref[1] + last_re

    both = jnp.concatenate([held_ref[0], held_ref[1]], axis=1)
    result = dot3((tz_ref[0], tz_ref[1]), halves(both))
    with_cos, with_sin = result[:depth], result[depth:]
    re = with_cos[:, :width] - with_sin[:, width:]
    im = with_cos[:, width:] + with_sin[:, :width]
    result = dot3(halves(jnp.concatenate([re, im], axis=0)), (ty_ref[0], ty_ref[1]))
    with_cos, with_sin = result[:, :width], result[:, width:]
    owners, _, _, planes, _ = out_ref.shape
    re = with_cos[:depth] - with_sin[depth:]
    im = with_cos[depth:] + with_sin[:depth]
    out_ref[:, 0, 0] = re.reshape(owners, planes, width)
    out_ref[:, 1, 0] = im.reshape(owners, planes, width)


def inverse_x(in_ref, tx_ref, out_ref):
    out_ref[0] = dot3(halves(in_ref[0]), (tx_ref[0], tx_ref[1]), ((0,), (0,)))


def whole_block(array, memory_space=None):
    if memory_space is not None:
        return pl.BlockSpec(memory_space=memory_space)
    zeros = (0,) * array.ndim
    return pl.BlockSpec(array.shape, lambda *_: zeros)


def on_device(source_field, receiver_fields, weights, model, wedge_sizes, wedge_scales):
    shots = lax.axis_size("shot")
    slabs = lax.axis_size("slab")
    shot = lax.axis_index("shot")
    slab = lax.axis_index("slab")
    devices = shots * slabs
    members, local, height, width = receiver_fields.shape
    planes = model.shape[0]
    depth = local * slabs
    slots = width // 2 // devices
    rows = width // shots
    part = local // CHUNKS
    params = functools.partial(pltpu.CompilerParams, vmem_limit_bytes=60 * 1024 * 1024)

    tx = host_halves(x_table(shots, slabs, width))
    ty = host_halves(np.concatenate(circle(np.arange(height), np.arange(height), height), axis=1))
    chunk_order = np.arange(depth).reshape(slabs, CHUNKS, part).transpose(1, 0, 2).reshape(-1)
    owner_order = np.arange(depth).reshape(slabs, shots, planes).transpose(1, 0, 2).reshape(-1)
    wavenumbers = np.arange(depth)
    tz = host_halves(np.concatenate(circle(wavenumbers, chunk_order, depth), axis=0))
    tz_back = host_halves(np.concatenate(circle(owner_order, wavenumbers, depth), axis=0))

    shot_index = shot.astype(jnp.int32).reshape(1)
    received = []
    for chunk in range(CHUNKS):
        first = chunk * part

        def model_block(z, sign, own, first=first):
            return (jnp.clip(z + first - own[0] * planes, 0, planes - 1), 0, 0)

        along_x = pl.pallas_call(
            functools.partial(forward_x, shots, planes, first),
            out_shape=jax.ShapeDtypeStruct((shots, part, rows, height), F32),
            grid_spec=pltpu.PrefetchScalarGridSpec(
                num_scalar_prefetch=2,
                grid=(part,),
                in_specs=[
                    pl.BlockSpec((1, height, width), lambda z, *_, first=first: (z + first, 0, 0)),
                    pl.BlockSpec(
                        (members, 1, height, width), lambda z, *_, first=first: (0, z + first, 0, 0)
                    ),
                    pl.BlockSpec((1, height, width), model_block),
                    whole_block(tx),
                ],
                out_specs=pl.BlockSpec((shots, 1, rows, height), lambda z, *_: (0, z, 0, 0)),
            ),
            compiler_params=params(),
            cost_estimate=pl.CostEstimate(
                flops=6 * part * height * width * width,
                bytes_accessed=part * height * width * 12,
                transcendentals=0,
            ),
        )(weights, shot_index, source_field[0], receiver_fields, model, tx)
        summed = lax.psum_scatter(along_x, "shot", scatter_dimension=0, tiled=True)[0]
        batch = min(part, 4)
        along_y = pl.pallas_call(
            functools.partial(forward_y, slabs),
            out_shape=jax.ShapeDtypeStruct((slabs, part, 2, slots, height), F32),
            grid=(part // batch,),
            in_specs=[
                pl.BlockSpec((batch, rows, height), lambda z: (z, 0, 0)),
                whole_block(ty),
            ],
            out_specs=pl.BlockSpec(
                (slabs, batch, 2, slots, height), lambda z: (0, z, 0, 0, 0)
            ),
            compiler_params=params(),
            cost_estimate=pl.CostEstimate(
                flops=12 * part * rows * height * height,
                bytes_accessed=part * rows * height * 8,
                transcendentals=0,
            ),
        )(summed, ty)
        gathered = lax.all_to_all(along_y, "slab", split_axis=0, concat_axis=0, tiled=True)
        received.append(
            jnp.transpose(
                gathered.reshape(slabs * part, 2, slots, height), (1, 2, 0, 3)
            )
        )

    packed = ((shot == 0) & (slab == 0)).astype(jnp.int32).reshape(1)
    spectrum, middle, power = pl.pallas_call(
        functools.partial(forward_z, slots),
        out_shape=(
            jax.ShapeDtypeStruct((slots, 2, depth, height), F32),
            jax.ShapeDtypeStruct((2, depth, height), F32),
            jax.ShapeDtypeStruct((slots + 1,), F32),
        ),
        grid=(slots,),
        in_specs=[whole_block(packed, pltpu.SMEM), whole_block(tz)]
        + [
            pl.BlockSpec((2, 1, slabs * part, height), lambda k: (0, k, 0, 0))
            for _ in received
        ],
        out_specs=(
            pl.BlockSpec((1, 2, depth, height), lambda k: (k, 0, 0, 0)),
            pl.BlockSpec((2, depth, height), lambda k: (0, 0, 0)),
            pl.BlockSpec(memory_space=pltpu.SMEM),
        ),
        compiler_params=params(),
    )(packed, tz, *received)

    ends = jnp.cumsum(wedge_sizes)
    starts = ends - wedge_sizes

    def members_of(columns):
        return (
            (columns[:, None] >= starts[None, :]) & (columns[:, None] < ends[None, :])
        ).astype(F32)

    columns = (shot * slabs + slab) * slots + lax.iota(jnp.int32, slots)
    columns = jnp.concatenate([columns, jnp.full((1,), width // 2, jnp.int32)])
    paired = (width - columns) % width
    here, there = members_of(columns), members_of(paired)
    counted = here + jnp.where(paired == columns, 0.0, 1.0)[:, None] * there
    own_power = jnp.dot(power, counted, precision=HIGHEST)
    everywhere = jnp.broadcast_to(own_power[None, :], (devices, own_power.shape[0]))
    wedge_power = jnp.sum(
        lax.all_to_all(everywhere, ("shot", "slab"), split_axis=0, concat_axis=0, tiled=True), axis=0
    )
    entries = wedge_sizes.astype(F32) * (depth * height)
    heights = wedge_scales * jnp.sqrt(wedge_power / entries + EPSILON)
    levels = jnp.stack(
        [
            jnp.dot(here, heights, precision=HIGHEST),
            jnp.dot(there, heights, precision=HIGHEST),
        ]
    )
    scale = jnp.where(paired == columns, 0.5, 1.0) * (1.0 / (depth * height * width))

    returned = pl.pallas_call(
        functools.partial(shrink_back, slots),
        out_shape=jax.ShapeDtypeStruct((devices, 2, slots, planes, height), F32),
        grid=(slots,),
        in_specs=[
            whole_block(levels, pltpu.SMEM),
            whole_block(scale, pltpu.SMEM),
            whole_block(tz_back),
            whole_block(ty),
            pl.BlockSpec((1, 2, depth, height), lambda k: (k, 0, 0, 0)),
            whole_block(middle),
        ],
        out_specs=pl.BlockSpec((devices, 2, 1, planes, height), lambda k: (0, 0, k, 0, 0)),
        scratch_shapes=[pltpu.VMEM((2, depth, height), F32)],
        compiler_params=params(),
    )(levels, scale, tz_back, ty, spectrum, middle)

    cleaned = lax.all_to_all(
        returned, ("shot", "slab"), split_axis=0, concat_axis=0, tiled=True
    )
    cleaned = jnp.transpose(cleaned.reshape(width, planes, height), (1, 0, 2))
    return pl.pallas_call(
        inverse_x,
        out_shape=jax.ShapeDtypeStruct((planes, height, width), F32),
        grid=(planes,),
        in_specs=[
            pl.BlockSpec((1, width, height), lambda z: (z, 0, 0)),
            whole_block(tx),
        ],
        out_specs=pl.BlockSpec((1, height, width), lambda z: (z, 0, 0)),
        compiler_params=params(),
    )(cleaned, tx)


def solution(mesh):
    placed = (
        P("shot", "slab", None, None),
        P("shot", "slab", None, None),
        P("shot"),
        P(("slab", "shot"), None, None),
        P(),
        P(),
    )
    return jax.shard_map(
        on_device,
        mesh=mesh,
        in_specs=placed,
        out_specs=P(("slab", "shot"), None, None),
        check_vma=False,
    )
```

```python
import functools
import math

import jax
import jax.numpy as jnp
import numpy as np
from jax import lax
from jax.experimental import pallas as pl
from jax.experimental.pallas import tpu as pltpu
from jax.sharding import PartitionSpec as P

STEP_SIZE = 0.25
EPSILON = 1e-06
HIGHEST = lax.Precision.HIGHEST
CHUNKS = (1, 5, 2)
F32 = jnp.float32
BF16 = jnp.bfloat16


def halves(x):
    high = x.astype(BF16)
    return high, (x - high.astype(F32)).astype(BF16)


def host_halves(table):
    table = table.astype(np.float32)
    high = table.astype(BF16)
    low = (table - high.astype(np.float32)).astype(BF16)
    return jnp.asarray(np.stack([high, low]))


def dot3(a, b, dims=((1,), (0,))):
    product = functools.partial(
        lax.dot_general, dimension_numbers=(dims, ((), ())), preferred_element_type=F32
    )
    return product(a[0], b[0]) + (product(a[0], b[1]) + product(a[1], b[0]))


def circle(rows, columns, length):
    angle = (np.outer(rows, columns) % length) * (2.0 * np.pi / length)
    return np.cos(angle), np.sin(angle)


def device_halves(rows, columns, length, axis):
    angle = (rows[:, None] * columns[None, :] % length).astype(F32) * (2.0 * np.pi / length)
    table = jnp.concatenate([jnp.cos(angle), jnp.sin(angle)], axis=axis)
    high = lax.reduce_precision(table, 8, 7)
    return jnp.stack([high.astype(BF16), (table - high).astype(BF16)])


def x_table(shots, slabs, width):
    slots = width // 2 // (shots * slabs)
    cosine, sine = circle(np.arange(width // 2), np.arange(width), width)
    sine = -sine
    sine[0] = 1.0 - 2.0 * (np.arange(width) % 2)
    shape = (shots * slabs, slots, width)
    return np.stack([cosine.reshape(shape), sine.reshape(shape)], axis=1).reshape(width, width)


def forward_x(shots, planes, first, sign_ref, shot_ref, source_ref, recv_ref, model_ref, tx_ref, out_ref):
    encoded = jnp.zeros(source_ref.shape[1:], F32)
    for member in range(recv_ref.shape[0]):
        encoded = encoded + sign_ref[member].astype(F32) * recv_ref[member, 0].astype(F32)
    plane = pl.program_id(0) + first
    own = (plane // planes == shot_ref[0]).astype(F32)
    part = own * model_ref[0].astype(F32) - STEP_SIZE * (source_ref[0].astype(F32) * encoded)
    result = dot3((tx_ref[0], tx_ref[1]), halves(part), ((1,), (1,)))
    rows = result.shape[0] // shots
    for shot in range(shots):
        out_ref[shot, 0] = result[shot * rows : (shot + 1) * rows]


def forward_y(slabs, in_ref, ty_ref, out_ref):
    depth, rows, width = in_ref.shape
    slots = rows // slabs // 2
    result = dot3(halves(in_ref[...].reshape(depth * rows, width)), (ty_ref[0], ty_ref[1]))
    with_cos, with_sin = result[:, :width], result[:, width:]
    for z in range(depth):
        for slab in range(slabs):
            re = z * rows + slab * 2 * slots
            im = re + slots
            out_ref[slab, z, 0] = with_cos[re : re + slots] + with_sin[im : im + slots]
            out_ref[slab, z, 1] = with_cos[im : im + slots] - with_sin[re : re + slots]


def forward_z(slots, packed_ref, tz_ref, *refs):
    count = len(CHUNKS)
    pieces, (out_ref, middle_ref, power_ref) = refs[:count], refs[count:]
    slot = pl.program_id(0)
    depth = tz_ref.shape[2]

    def load(part):
        return jnp.concatenate([piece[part, 0] for piece in pieces], axis=0)

    def transform(re, im):
        width = re.shape[1]
        result = dot3((tz_ref[0], tz_ref[1]), halves(jnp.concatenate([re, im], axis=1)))
        with_cos, with_sin = result[:depth], result[depth:]
        return (
            with_cos[:, :width] + with_sin[:, width:],
            with_cos[:, width:] - with_sin[:, :width],
        )

    re_in, im_in = load(0), load(1)
    re, im = transform(re_in, im_in)
    out_ref[0, 0] = re
    out_ref[0, 1] = im
    power_ref[slot] = jnp.sum(re * re + im * im)

    @pl.when(slot == 0)
    def _():
        width = re.shape[1]
        sums = lax.broadcasted_iota(jnp.int32, (width, width), 0) + lax.broadcasted_iota(
            jnp.int32, (width, width), 1
        )
        mirror = ((sums == 0) | (sums == width)).astype(F32).astype(BF16)

        def flip(x):
            high, low = halves(x)
            return jnp.dot(high, mirror, preferred_element_type=F32) + jnp.dot(
                low, mirror, preferred_element_type=F32
            )

        other_re, other_im = transform(flip(re_in), -flip(im_in))
        flag = packed_ref[0] != 0
        first_re = jnp.where(flag, 0.5 * (re + other_re), re)
        first_im = jnp.where(flag, 0.5 * (im + other_im), im)
        last_re = jnp.where(flag, 0.5 * (im - other_im), 0.0)
        last_im = jnp.where(flag, 0.5 * (other_re - re), 0.0)
        out_ref[0, 0] = first_re
        out_ref[0, 1] = first_im
        middle_ref[0] = last_re
        middle_ref[1] = last_im
        power_ref[0] = jnp.sum(first_re * first_re + first_im * first_im)
        power_ref[slots] = jnp.sum(last_re * last_re + last_im * last_im)


def shrink_back(low, slots, level_ref, scale_ref, tz_ref, ty_ref, spec_ref, middle_ref, out_ref, held_ref):
    slot = pl.program_id(0) + low
    depth, width = spec_ref.shape[2:]

    def shrunk(re, im, index):
        magnitude = jnp.sqrt(re * re + im * im)
        total = 0.0
        for side in range(2):
            level = level_ref[side, index]
            total = total + jnp.maximum(magnitude - level, 0.0) / jnp.maximum(magnitude, level)
        total = total * scale_ref[index]
        return re * total, im * total

    re, im = shrunk(spec_ref[0, 0], spec_ref[0, 1], slot)
    held_ref[0] = re
    held_ref[1] = im

    @pl.when(slot == 0)
    def _():
        last_re, last_im = shrunk(middle_ref[0], middle_ref[1], slots)
        held_ref[0] = held_ref[0] - last_im
        held_ref[1] = held_ref[1] + last_re

    both = jnp.concatenate([held_ref[0], held_ref[1]], axis=1)
    result = dot3((tz_ref[0], tz_ref[1]), halves(both))
    with_cos, with_sin = result[:depth], result[depth:]
    re = with_cos[:, :width] - with_sin[:, width:]
    im = with_cos[:, width:] + with_sin[:, :width]
    result = dot3(halves(jnp.concatenate([re, im], axis=0)), (ty_ref[0], ty_ref[1]))
    with_cos, with_sin = result[:, :width], result[:, width:]
    owners, _, _, planes, _ = out_ref.shape
    re = with_cos[:depth] - with_sin[depth:]
    im = with_cos[depth:] + with_sin[:depth]
    out_ref[:, 0, 0] = re.reshape(owners, planes, width)
    out_ref[:, 1, 0] = im.reshape(owners, planes, width)


def inverse_x(*refs):
    count = len(refs) // 2
    total = 0.0
    for in_ref, tx_ref in zip(refs[:count], refs[count : 2 * count]):
        total = total + dot3(halves(in_ref[0]), (tx_ref[0], tx_ref[1]), ((0,), (0,)))
    refs[-1][0] = total


def whole_block(array, memory_space=None):
    if memory_space is not None:
        return pl.BlockSpec(memory_space=memory_space)
    zeros = (0,) * array.ndim
    return pl.BlockSpec(array.shape, lambda *_: zeros)


def on_device(source_field, receiver_fields, weights, model, wedge_sizes, wedge_scales):
    shots = lax.axis_size("shot")
    slabs = lax.axis_size("slab")
    shot = lax.axis_index("shot")
    slab = lax.axis_index("slab")
    devices = shots * slabs
    members, local, height, width = receiver_fields.shape
    planes = model.shape[0]
    depth = local * slabs
    slots = width // 2 // devices
    rows = width // shots
    parts = [local * share // sum(CHUNKS) for share in CHUNKS]
    params = functools.partial(pltpu.CompilerParams, vmem_limit_bytes=60 * 1024 * 1024)

    tx = host_halves(x_table(shots, slabs, width))
    firsts = [sum(parts[:chunk]) for chunk in range(len(parts))]
    depth_index = np.arange(depth, dtype=np.int32)
    by_slab = depth_index.reshape(slabs, local)
    chunk_order = np.concatenate(
        [by_slab[:, a : a + part].reshape(-1) for a, part in zip(firsts, parts)]
    )
    owner_order = depth_index.reshape(slabs, shots, planes).transpose(1, 0, 2).reshape(-1)

    shot_index = shot.astype(jnp.int32).reshape(1)
    received, sums = [], []
    for chunk, (first, part) in enumerate(zip(firsts, parts)):

        def model_block(z, sign, own, first=first):
            return (jnp.clip(z + first - own[0] * planes, 0, planes - 1), 0, 0)

        along_x = pl.pallas_call(
            functools.partial(forward_x, shots, planes, first),
            out_shape=jax.ShapeDtypeStruct((shots, part, rows, height), F32),
            grid_spec=pltpu.PrefetchScalarGridSpec(
                num_scalar_prefetch=2,
                grid=(part,),
                in_specs=[
                    pl.BlockSpec((1, height, width), lambda z, *_, first=first: (z + first, 0, 0)),
                    pl.BlockSpec(
                        (members, 1, height, width), lambda z, *_, first=first: (0, z + first, 0, 0)
                    ),
                    pl.BlockSpec((1, height, width), model_block),
                    whole_block(tx),
                ],
                out_specs=pl.BlockSpec((shots, 1, rows, height), lambda z, *_: (0, z, 0, 0)),
            ),
            compiler_params=params(),
            cost_estimate=pl.CostEstimate(
                flops=6 * part * height * width * width,
                bytes_accessed=part * height * width * 12,
                transcendentals=0,
            ),
        )(weights, shot_index, source_field[0], receiver_fields, model, tx)
        along_x, shot_index = lax.optimization_barrier((along_x, shot_index))
        if chunk == 0:
            order = (np.arange(height, dtype=np.int32), depth_index, chunk_order, owner_order)
            along_x, order = lax.optimization_barrier((along_x, order))
            height_index, plain, by_chunk, by_owner = order
            ty = device_halves(height_index, height_index, height, 1)
            tz = device_halves(plain, by_chunk, depth, 0)
            tz_back = device_halves(by_owner, plain, depth, 0)
        sums.append(lax.psum_scatter(along_x, "shot", scatter_dimension=0, tiled=True)[0])

    for part, summed in zip(parts, sums):
        batch = math.gcd(part, 4)
        along_y = pl.pallas_call(
            functools.partial(forward_y, slabs),
            out_shape=jax.ShapeDtypeStruct((slabs, part, 2, slots, height), F32),
            grid=(part // batch,),
            in_specs=[
                pl.BlockSpec((batch, rows, height), lambda z: (z, 0, 0)),
                whole_block(ty),
            ],
            out_specs=pl.BlockSpec(
                (slabs, batch, 2, slots, height), lambda z: (0, z, 0, 0, 0)
            ),
            compiler_params=params(),
            cost_estimate=pl.CostEstimate(
                flops=12 * part * rows * height * height,
                bytes_accessed=part * rows * height * 8,
                transcendentals=0,
            ),
        )(summed, ty)
        gathered = lax.all_to_all(along_y, "slab", split_axis=0, concat_axis=0, tiled=True)
        received.append(
            jnp.transpose(
                gathered.reshape(slabs * part, 2, slots, height), (1, 2, 0, 3)
            )
        )

    packed = ((shot == 0) & (slab == 0)).astype(jnp.int32).reshape(1)
    spectrum, middle, power = pl.pallas_call(
        functools.partial(forward_z, slots),
        out_shape=(
            jax.ShapeDtypeStruct((slots, 2, depth, height), F32),
            jax.ShapeDtypeStruct((2, depth, height), F32),
            jax.ShapeDtypeStruct((slots + 1,), F32),
        ),
        grid=(slots,),
        in_specs=[whole_block(packed, pltpu.SMEM), whole_block(tz)]
        + [
            pl.BlockSpec((2, 1, slabs * part, height), lambda k: (0, k, 0, 0))
            for part in parts
        ],
        out_specs=(
            pl.BlockSpec((1, 2, depth, height), lambda k: (k, 0, 0, 0)),
            pl.BlockSpec((2, depth, height), lambda k: (0, 0, 0)),
            pl.BlockSpec(memory_space=pltpu.SMEM),
        ),
        compiler_params=params(),
    )(packed, tz, *received)

    ends = jnp.cumsum(wedge_sizes)
    starts = ends - wedge_sizes

    def members_of(columns):
        return (
            (columns[:, None] >= starts[None, :]) & (columns[:, None] < ends[None, :])
        ).astype(F32)

    columns = (shot * slabs + slab) * slots + lax.iota(jnp.int32, slots)
    columns = jnp.concatenate([columns, jnp.full((1,), width // 2, jnp.int32)])
    paired = (width - columns) % width
    here, there = members_of(columns), members_of(paired)
    counted = here + jnp.where(paired == columns, 0.0, 1.0)[:, None] * there
    own_power = jnp.dot(power, counted, precision=HIGHEST)
    everywhere = jnp.broadcast_to(own_power[None, :], (devices, own_power.shape[0]))
    wedge_power = jnp.sum(
        lax.all_to_all(everywhere, ("shot", "slab"), split_axis=0, concat_axis=0, tiled=True), axis=0
    )
    entries = wedge_sizes.astype(F32) * (depth * height)
    heights = wedge_scales * jnp.sqrt(wedge_power / entries + EPSILON)
    levels = jnp.stack(
        [
            jnp.dot(here, heights, precision=HIGHEST),
            jnp.dot(there, heights, precision=HIGHEST),
        ]
    )
    scale = jnp.where(paired == columns, 0.5, 1.0) * (1.0 / (depth * height * width))

    cut = slots // 4
    groups = [(0, cut), (cut, slots)] if cut else [(0, slots)]
    tables = lax.optimization_barrier((tx, along_y))[0].reshape(2, devices, 2, slots, width)
    cleaned, sides = [], []
    for low, high in groups:
        count = high - low
        returned = pl.pallas_call(
            functools.partial(shrink_back, low, slots),
            out_shape=jax.ShapeDtypeStruct((devices, 2, count, planes, height), F32),
            grid=(count,),
            in_specs=[
                whole_block(levels, pltpu.SMEM),
                whole_block(scale, pltpu.SMEM),
                whole_block(tz_back),
                whole_block(ty),
                pl.BlockSpec((1, 2, depth, height), lambda k, low=low: (k + low, 0, 0, 0)),
                whole_block(middle),
            ],
            out_specs=pl.BlockSpec((devices, 2, 1, planes, height), lambda k: (0, 0, k, 0, 0)),
            scratch_shapes=[pltpu.VMEM((2, depth, height), F32)],
            compiler_params=params(),
            cost_estimate=pl.CostEstimate(
                flops=12 * count * depth * height * (depth + height),
                bytes_accessed=count * depth * height * 16,
                transcendentals=count * depth * height,
            ),
        )(levels, scale, tz_back, ty, spectrum, middle)
        back = lax.all_to_all(
            returned, ("shot", "slab"), split_axis=0, concat_axis=0, tiled=True
        )
        terms = devices * 2 * count
        cleaned.append(jnp.transpose(back.reshape(terms, planes, height), (1, 0, 2)))
        sides.append(tables[:, :, :, low:high].reshape(2, terms, width))

    return pl.pallas_call(
        inverse_x,
        out_shape=jax.ShapeDtypeStruct((planes, height, width), F32),
        grid=(planes,),
        in_specs=[
            pl.BlockSpec((1,) + piece.shape[1:], lambda z: (z, 0, 0)) for piece in cleaned
        ]
        + [whole_block(side) for side in sides],
        out_specs=pl.BlockSpec((1, height, width), lambda z: (z, 0, 0)),
        compiler_params=params(),
    )(*cleaned, *sides)


def solution(mesh):
    placed = (
        P("shot", "slab", None, None),
        P("shot", "slab", None, None),
        P("shot"),
        P(("slab", "shot"), None, None),
        P(),
        P(),
    )
    return jax.shard_map(
        on_device,
        mesh=mesh,
        in_specs=placed,
        out_specs=P(("slab", "shot"), None, None),
        check_vma=False,
    )
```
